1024 devices in a mesh: blk: 128 (over z, y_lo, core), dx: 2 (over y_hi), dy: 4 (over x).
Axes of the slice: x: 4, y: 8 (y_hi: 2, y_lo: 4; y = y_hi * 4 + y_lo), z: 16, core: 2. Of those that a mesh axis runs over, the one named last changes fastest.
Arguments:
- orbitals: bfloat16 [16384, 8, 32, 128], P('blk', 'dx', 'dy'), may hold values from -6 to 6
- coupling: float32 [8, 32, 128], P('dx', 'dy'), may hold values from 0.3 to 3
- pot_grad: float32 [3, 8, 32, 128], P(None, 'dx', 'dy'), may hold values from -6 to 6
Outputs:
- spin_orbit: float32 [3, 5, 16384, 128], P(None, None, ('blk', 'dx', 'dy'))
The draws below stay inside these ranges and needn't reach their ends.
All inputs are finite; a program needn't handle non-finite values.
Results may differ from the reference program's by a relative error of at most 0.0029.
Values may be sent and summed in bfloat16 or wider, within the bound.
A program may use at most 32 MiB of HBM per device.

```python
import math
import jax
import jax.numpy as jnp
from jax import lax

P_SIZE = 128
HALF = 2
NSTATES = 16384
NX = 8
NY = 32
NZ = 128
N_BLK = 128


def steps_of(rng, dims, pieces, low, largest):
    loudness, own = 1.0, jax.random.fold_in(rng, 6)
    for position, parts in pieces:
        steps = jnp.exp(jax.random.uniform(jax.random.fold_in(own, position), (parts,), jnp.float32, low / len(pieces), largest / len(pieces)))
        loudness = loudness * jnp.repeat(steps, dims[position] // parts).reshape([-1 if axis == position else 1 for axis in range(len(dims))])
    return loudness


def scatter_about(own_key, extent, width, bound, cuts=(), held_as=jnp.bfloat16):
    gain = steps_of(own_key, extent, cuts, -0.22, 0.18) if cuts else 1.0
    drawn = jax.random.normal(own_key, extent, jnp.float32) * width * gain
    return jnp.minimum(jnp.maximum(drawn, -bound), bound).astype(held_as)


def setup_inputs(seed: int = 0) -> dict:
    streams_of = jax.random.split(jax.random.key(seed), 4)
    orbitals = scatter_about(streams_of[0], (NSTATES, NX, NY, NZ), 1.0, 6.0, ((0, 128), (1, 2), (2, 4)))
    coupling = jnp.clip(jnp.exp(math.log(3.0) - 2.3025851 * jax.random.uniform(streams_of[1], (NX, NY, NZ), jnp.float32) ** steps_of(streams_of[1], (NX, NY, NZ), ((0, 2), (1, 4)), -0.2, 0.2)), 0.3, 3.0)
    pot_grad = scatter_about(streams_of[2], (3, NX, NY, NZ), 1.0, 6.0, ((1, 2), (2, 4)), jnp.float32)
    return {"orbitals": orbitals, "coupling": coupling, "pot_grad": pot_grad}


def reference(orbitals, coupling, pot_grad):
    cell_count = NX * NY * NZ
    weight_scale = 1.0 / math.sqrt(cell_count)
    coeff_field = coupling[None] * pot_grad
    coeff_one, coeff_two, coeff_three = (coeff_field[0], coeff_field[1], coeff_field[2])
    flat = orbitals.reshape(N_BLK, P_SIZE, cell_count)

    def one_panel(b):
        panel = lax.dynamic_index_in_dim(flat, b, 0, keepdims=False)
        field_f32 = panel.reshape(P_SIZE, NX, NY, NZ).astype(jnp.float32)
        gradient = [0.5 * (jnp.roll(field_f32, -1, axis=a) - jnp.roll(field_f32, 1, axis=a)) for a in (1, 2, 3)]
        cross_one = coeff_two * gradient[2] - coeff_three * gradient[1]
        cross_two = coeff_three * gradient[0] - coeff_one * gradient[2]
        cross_three = coeff_one * gradient[1] - coeff_two * gradient[0]
        cross_field = jnp.stack([cross_one, cross_two, cross_three]).astype(jnp.bfloat16)
        cross_field = cross_field.reshape(3, P_SIZE, cell_count).astype(jnp.float32)
        tile_list = []
        for t in range(2 * HALF + 1):
            other_index = ((b + t - HALF) % N_BLK).astype(jnp.int32)
            other = lax.dynamic_index_in_dim(flat, other_index, 0, keepdims=False).astype(jnp.float32)
            tile_list.append(jnp.einsum('kjc,ic->kji', cross_field, other))
        return jnp.stack(tile_list, 1) * weight_scale
    every_panel = lax.map(one_panel, jnp.arange(N_BLK, dtype=jnp.int32))
    return every_panel.transpose(1, 2, 0, 3, 4).reshape(3, 2 * HALF + 1, N_BLK * P_SIZE, P_SIZE)
```

```python
import functools
import math

import jax
import jax.numpy as jnp
from jax import lax
from jax.experimental import pallas as pl
from jax.experimental.pallas import tpu as pltpu
from jax.sharding import PartitionSpec as P

MESH = pl.DeviceIdType.MESH
BF16 = jnp.bfloat16
F32 = jnp.float32
NT = (((1,), (1,)), ((), ()))


def wide(value):
    return jnp.concatenate([value[r] for r in range(value.shape[0])], axis=1)


def kernel(
    n_blk, scale,
    psi, coupling, pot_grad, out,
    pad, cf, cfx, cfy, ct, uv, far, acc, stage, from_dy, half, from_dx, from_one, from_two,
    load_sem, xs, xr, ys, yr, cxs, cxr, cys, cyr, chain_s, chain_r, core_s, core_r,
    sum_s, sum_r, home_s, home_r,
):
    b, dx, dy = lax.axis_index("blk"), lax.axis_index("dx"), lax.axis_index("dy")
    core = lax.rem(b, 2)

    def at(block, x, y):
        return (lax.rem(block + n_blk, n_blk), x, lax.rem(y + 4, 4))

    partner = at(b, 1 - dx, dy)
    mate = at(b + 1 - 2 * core, dx, dy)

    def remote(src, dst, send, recv, device):
        return pltpu.make_async_remote_copy(
            src_ref=src, dst_ref=dst, send_sem=send, recv_sem=recv, device_id=device, device_id_type=MESH
        )

    barrier = pltpu.get_barrier_semaphore()
    sources = [partner, mate, at(b + 2, dx, dy)]
    sources += [at(b, dx, dy + o) for o in (1, 2, 3)]
    sources += [at(b - d, x, dy) for d in (1, 2) for x in (0, 1)]
    for device in sources:
        pl.semaphore_signal(barrier, inc=1, device_id=device, device_id_type=MESH)

    own = pad.at[pl.ds(1, 4), pl.ds(1, 8)]
    load = pltpu.make_async_copy(psi, own, load_sem)
    load.start()
    for k in range(3):
        cf[k] = coupling[...] * pot_grad[k]
    load.wait()
    pl.semaphore_wait(barrier, len(sources))

    x_copies = [
        remote(pad.at[4, pl.ds(1, 8)], pad.at[0, pl.ds(1, 8)], xs.at[0], xr.at[0], partner),
        remote(pad.at[1, pl.ds(1, 8)], pad.at[5, pl.ds(1, 8)], xs.at[1], xr.at[1], partner),
        remote(cf.at[:, 3], cfx.at[:, 0], cxs.at[0], cxr.at[0], partner),
        remote(cf.at[:, 0], cfx.at[:, 1], cxs.at[1], cxr.at[1], partner),
    ]
    y_copies = [
        remote(pad.at[pl.ds(1, 4), 8], pad.at[pl.ds(1, 4), 0], ys.at[0], yr.at[0], at(b, dx, dy + 1)),
        remote(pad.at[pl.ds(1, 4), 1], pad.at[pl.ds(1, 4), 9], ys.at[1], yr.at[1], at(b, dx, dy - 1)),
        remote(cf, cfy.at[0], cys.at[0], cyr.at[0], at(b, dx, dy + 1)),
        remote(cf, cfy.at[1], cys.at[1], cyr.at[1], at(b, dx, dy - 1)),
    ]
    for copy in x_copies[2:] + y_copies[2:] + y_copies[:2] + x_copies[:2]:
        copy.start()
    order = (1, 2, 0, 3)
    chain = [
        remote(pad.at[l + 1, pl.ds(1, 8)], far.at[1, l], chain_s.at[l], chain_r.at[l], at(b - 2, dx, dy))
        for l in range(4)
    ]
    hand = [remote(pad.at[l + 1, pl.ds(1, 8)], far.at[0, l], core_s.at[l], core_r.at[l], mate) for l in range(4)]
    pass_on = [remote(far.at[1, l], far.at[0, l], core_s.at[l], core_r.at[l], mate) for l in range(4)]
    for l in order:
        chain[l].start()

    @pl.when(core == 1)
    def _():
        for l in order:
            hand[l].start()

    for copy in x_copies[2:] + y_copies[2:]:
        copy.wait_recv()
    row = lax.broadcasted_iota(jnp.int32, (8, 128), 0)
    for l in range(4):
        here = [cf[k, l] * 0.5 for k in range(3)]
        for k in range(3):
            ct[k, l] = here[k]
        up = [(cf[k, l + 1] if l < 3 else cfx[k, 1]) * 0.5 for k in range(3)]
        down = [(cf[k, l - 1] if l > 0 else cfx[k, 0]) * 0.5 for k in range(3)]
        ct[3, l] = up[1]
        ct[4, l] = up[2]
        ct[5, l] = down[1]
        ct[6, l] = down[2]
        for n, k in ((7, 0), (8, 2)):
            ct[n, l] = jnp.where(row == 7, pltpu.roll(cfy[1, k, l] * 0.5, 7, 0), pltpu.roll(here[k], 7, 0))
            ct[n + 2, l] = jnp.where(row == 0, pltpu.roll(cfy[0, k, l] * 0.5, 1, 0), pltpu.roll(here[k], 1, 0))
        for n, k in ((11, 0), (12, 1)):
            ct[n, l] = pltpu.roll(here[k], 127, 1)
            ct[n + 2, l] = pltpu.roll(here[k], 1, 1)

    rows = 32

    def fields_of(l):
        def one_row(r, carry):
            c = [jnp.broadcast_to(ct[n, l, pl.ds(r, 1), :], (rows, 128)) for n in range(15)]
            c1, c2, c3, c2xp, c3xp, c2xm, c3xm, c1yp, c3yp, c1ym, c3ym, c1zp, c2zp, c1zm, c2zm = c
            for j in range(128 // rows):
                part = pl.ds(j * rows, rows)
                mid = pad[l + 1, r + 1, part, :].astype(F32)
                xp = pad[l + 2, r + 1, part, :].astype(F32)
                xm = pad[l, r + 1, part, :].astype(F32)
                yp = pad[l + 1, r + 2, part, :].astype(F32)
                ym = pad[l + 1, r, part, :].astype(F32)
                zp = pltpu.roll(mid, 127, 1)
                zm = pltpu.roll(mid, 1, 1)
                g1, g2, g3 = xp - xm, yp - ym, zp - zm
                uv[0, l, r, part, :] = (c2 * g3 - c3 * g2).astype(BF16)
                uv[1, l, r, part, :] = (c3 * g1 - c1 * g3).astype(BF16)
                uv[2, l, r, part, :] = (c1 * g2 - c2 * g1).astype(BF16)
                uv[3, l, r, part, :] = ((c3yp * yp - c3ym * ym) - (c2zp * zp - c2zm * zm)).astype(BF16)
                uv[4, l, r, part, :] = ((c1zp * zp - c1zm * zm) - (c3xp * xp - c3xm * xm)).astype(BF16)
                uv[5, l, r, part, :] = ((c2xp * xp - c2xm * xm) - (c1yp * yp - c1ym * ym)).astype(BF16)
            return carry

        lax.fori_loop(0, 8, one_row, 0)

    def left(k, l):
        return wide(uv[k, l])

    def add_own(l, first):
        right = wide(pad[l + 1, pl.ds(1, 8)])
        for k in range(3):
            part = lax.dot_general(left(k, l), right, NT, preferred_element_type=F32)
            acc[k] = part if first else acc[k] + part

    def add_far(l, first):
        q = jnp.concatenate([wide(far[0, l]), wide(far[1, l])], axis=0)
        for k in range(3):
            part = lax.dot_general(left(k, l), q, NT, preferred_element_type=F32)
            for side in range(2):
                piece = part[:, side * 128 : side * 128 + 128]
                t = 3 + 3 * side + k
                acc[t] = piece if first else acc[t] + piece
            part = lax.dot_general(q, left(3 + k, l), NT, preferred_element_type=F32)
            for side in range(2):
                piece = part[side * 128 : side * 128 + 128]
                t = 9 + 3 * side + k
                acc[t] = piece if first else acc[t] + piece

    def send_sums(tiles, group):
        for t in range(tiles.start, tiles.start + tiles.size):
            stage[t] = acc[t].astype(BF16).reshape(2, 4, 16, 128)
        copies = []
        for o in (1, 2, 3):
            to = lax.rem(dy + o, 4)
            copy = remote(
                stage.at[tiles, :, to], from_dy.at[o - 1, tiles],
                sum_s.at[group, o - 1], sum_r.at[group, o - 1], at(b, dx, dy + o),
            )
            copy.start()
            copies.append(copy)
        return copies

    def sums(t, x):
        total = acc[t, pl.ds(pl.multiple_of((x * 4 + dy) * 16, 16), 16), :]
        for o in range(3):
            total = total + from_dy[o, t, x].astype(F32)
        return total

    for copy in y_copies[:2]:
        copy.wait_recv()
    for n, l in enumerate(order):
        if l == 0:
            for copy in x_copies[:2]:
                copy.wait_recv()
        fields_of(l)
        add_own(l, n == 0)
    first_sums = send_sums(pl.ds(0, 3), 0)

    for n, l in enumerate(order):
        chain[l].wait_recv()

        @pl.when(core == 0)
        def _(l=l):
            pass_on[l].start()

        hand[l].wait_recv()
        add_far(l, n == 0)
    last_sums = send_sums(pl.ds(3, 12), 1)

    other = 1 - dx
    for copy in first_sums + last_sums:
        copy.wait_recv()
    for t in range(9):
        half[t] = sums(t, other)
    home = [remote(half.at[pl.ds(0, 9)], from_dx, home_s.at[0], home_r.at[0], partner)]
    home[0].start()
    for x in range(2):
        for k in range(3):
            half[9 + 6 * x + k] = sums(9 + k, x)
            half[12 + 6 * x + k] = sums(12 + k, x)
        one = remote(
            half.at[pl.ds(9 + 6 * x, 3)], from_one.at[dx], home_s.at[1 + x], home_r.at[1 + dx], at(b + 1, x, dy)
        )
        two = remote(
            half.at[pl.ds(12 + 6 * x, 3)], from_two.at[dx], home_s.at[3 + x], home_r.at[3 + dx], at(b + 2, x, dy)
        )
        one.start()
        two.start()
        home += [one, two]

    home[0].wait_recv()
    for k in range(3):
        for t in range(3):
            out[k, 2 + t] = (sums(3 * t + k, dx) + from_dx[3 * t + k]) * scale
    for x in range(2):
        arrived = remote(half.at[pl.ds(9, 3)], from_one.at[x], home_s.at[1 + x], home_r.at[1 + x], partner)
        arrived.wait_recv()
        arrived = remote(half.at[pl.ds(12, 3)], from_two.at[x], home_s.at[3 + x], home_r.at[3 + x], partner)
        arrived.wait_recv()
    for k in range(3):
        out[k, 1] = (from_one[0, k] + from_one[1, k]) * scale
        out[k, 0] = (from_two[0, k] + from_two[1, k]) * scale

    for copy in x_copies + y_copies + chain + first_sums + last_sums + home:
        copy.wait_send()
    for l in range(4):
        hand[l].wait_send()


def on_device(n_blk, scale, orbitals, coupling, pot_grad):
    psi = orbitals.transpose(1, 2, 0, 3)
    dma = pltpu.SemaphoreType.DMA
    vmem = pl.BlockSpec(memory_space=pltpu.VMEM)
    return pl.pallas_call(
        functools.partial(kernel, n_blk, scale),
        out_shape=jax.ShapeDtypeStruct((3, 5, 16, 128), F32),
        in_specs=[pl.BlockSpec(memory_space=pl.ANY), vmem, vmem],
        out_specs=vmem,
        scratch_shapes=[
            pltpu.VMEM((6, 10, 128, 128), BF16),
            pltpu.VMEM((3, 4, 8, 128), F32),
            pltpu.VMEM((3, 2, 8, 128), F32),
            pltpu.VMEM((2, 3, 4, 8, 128), F32),
            pltpu.VMEM((15, 4, 8, 128), F32),
            pltpu.VMEM((6, 4, 8, 128, 128), BF16),
            pltpu.VMEM((2, 4, 8, 128, 128), BF16),
            pltpu.VMEM((15, 128, 128), F32),
            pltpu.VMEM((15, 2, 4, 16, 128), BF16),
            pltpu.VMEM((3, 15, 2, 16, 128), BF16),
            pltpu.VMEM((21, 16, 128), F32),
            pltpu.VMEM((9, 16, 128), F32),
            pltpu.VMEM((2, 3, 16, 128), F32),
            pltpu.VMEM((2, 3, 16, 128), F32),
            dma, dma((2,)), dma((2,)), dma((2,)), dma((2,)), dma((2,)), dma((2,)), dma((2,)), dma((2,)),
            dma((4,)), dma((4,)), dma((4,)), dma((4,)),
            dma((2, 3)), dma((2, 3)), dma((5,)), dma((5,)),
        ],
        compiler_params=pltpu.CompilerParams(
            collective_id=0, has_side_effects=True, vmem_limit_bytes=56 * 1024 * 1024
        ),
    )(psi, coupling, pot_grad)


def solution(mesh):
    cells = 8 * 32 * 128
    in_specs = (P("blk", "dx", "dy", None), P("dx", "dy", None), P(None, "dx", "dy", None))
    out_specs = P(None, None, ("blk", "dx", "dy"), None)
    return jax.shard_map(
        functools.partial(on_device, mesh.shape["blk"], 1.0 / math.sqrt(cells)),
        mesh=mesh, in_specs=in_specs, out_specs=out_specs, check_vma=False,
    )
```

```python
import functools
import math

import jax
import jax.numpy as jnp
from jax import lax
from jax.experimental import pallas as pl
from jax.experimental.pallas import tpu as pltpu
from jax.sharding import PartitionSpec as P

MESH = pl.DeviceIdType.MESH
BF16 = jnp.bfloat16
F32 = jnp.float32
NT = (((1,), (1,)), ((), ()))


def wide(value):
    return jnp.concatenate([value[r] for r in range(value.shape[0])], axis=1)


def kernel(
    n_blk, scale,
    psi, coupling, pot_grad, out,
    flat, pad, cf, cfx, cfy, ct, uv, far, lent, acc, stage, from_dy, half, from_dx, from_one, from_two,
    xs, xr, ys, yr, cxs, cxr, cys, cyr, hand_s, lend_s, lend_r, chain_s, pass_s, far_r,
    sum_s, sum_r, home_s, home_r, late,
):
    b, dx, dy = lax.axis_index("blk"), lax.axis_index("dx"), lax.axis_index("dy")
    core = lax.rem(b, 2)

    def at(block, x, y):
        return (lax.rem(block + n_blk, n_blk), x, lax.rem(y + 4, 4))

    def is_root(device):
        return (device[0] == 0) & (device[1] == 0) & (device[2] == 0)

    partner = at(b, 1 - dx, dy)
    mate = at(b + 1 - 2 * core, dx, dy)
    above, below = at(b, dx, dy + 1), at(b, dx, dy - 1)

    def remote(src, dst, send, recv, device):
        return pltpu.make_async_remote_copy(
            src_ref=src, dst_ref=dst, send_sem=send, recv_sem=recv, device_id=device, device_id_type=MESH
        )

    friends = [partner] + [at(b, dx, dy + o) for o in (1, 2, 3)]
    friends += [at(b + d, x, dy) for d in (-2, -1, 1, 2) for x in (0, 1)]
    root = is_root((b, dx, dy))
    near = jnp.int32(0)
    for device in friends:
        near = near + is_root(device).astype(jnp.int32)
    barrier = pltpu.get_barrier_semaphore()

    @pl.when(jnp.logical_not(root))
    def _():
        for device in friends:
            pl.semaphore_signal(barrier, inc=1, device_id=device, device_id_type=MESH)

    for k in range(3):
        cf[k] = coupling[...] * pot_grad[k]

    for j in range(8):
        flat[pl.ds(j * 512, 512), :] = psi[pl.ds(j * 16, 16)].astype(F32).reshape(512, 128)
    for l in (0, 3, 1, 2):

        def turn(r, carry, l=l):
            pad[l + 1, r + 1] = flat[pl.ds(l * 8 + r, 128, stride=32), :].astype(BF16)
            return carry

        lax.fori_loop(0, 8, turn, 0)
    pl.semaphore_wait(barrier, len(friends) - near)

    @pl.when(root)
    def _():
        for device in friends:
            pl.semaphore_signal(late, inc=1, device_id=device, device_id_type=MESH)

    ends = pl.ds(1, 8)
    layers = pl.ds(1, 4)
    x_copies = [
        remote(pad.at[4, ends], pad.at[0, ends], xs.at[0], xr.at[0], partner),
        remote(pad.at[1, ends], pad.at[5, ends], xs.at[1], xr.at[1], partner),
    ]
    cx_copies = [
        remote(cf.at[:, 3], cfx.at[:, 0], cxs.at[0], cxr.at[0], partner),
        remote(cf.at[:, 0], cfx.at[:, 1], cxs.at[1], cxr.at[1], partner),
    ]
    y_copies = [
        remote(pad.at[layers, 8], pad.at[layers, 0], ys.at[0], yr.at[0], above),
        remote(pad.at[layers, 1], pad.at[layers, 9], ys.at[1], yr.at[1], below),
    ]
    cy_copies = [
        remote(cf, cfy.at[0], cys.at[0], cyr.at[0], above),
        remote(cf, cfy.at[1], cys.at[1], cyr.at[1], below),
    ]
    hand = [remote(pad.at[l + 1, ends], far.at[0, l], hand_s.at[l], far_r.at[0, l], mate) for l in range(4)]
    lend = [remote(pad.at[3 * i + 1, ends], lent.at[i], lend_s.at[i], lend_r.at[i], mate) for i in range(2)]

    def start_first(when):
        groups = [
            (partner, cx_copies + x_copies),
            (above, [cy_copies[0], y_copies[0]]),
            (below, [cy_copies[1], y_copies[1]]),
        ]
        for device, copies in groups:

            @pl.when(when(device))
            def _(copies=copies):
                for copy in copies:
                    copy.start()

        @pl.when(when(mate) & (core == 1))
        def _():
            for l in (1, 2, 0, 3):
                hand[l].start()

        @pl.when(when(mate) & (core == 0))
        def _():
            for copy in lend:
                copy.start()

    start_first(lambda device: jnp.logical_not(is_root(device)))

    row = lax.broadcasted_iota(jnp.int32, (8, 128), 0)

    def coefficients(l):
        here = [cf[k, l] * 0.5 for k in range(3)]
        for k in range(3):
            ct[k, l] = here[k]
        up = [(cf[k, l + 1] if l < 3 else cfx[k, 1]) * 0.5 for k in range(3)]
        down = [(cf[k, l - 1] if l > 0 else cfx[k, 0]) * 0.5 for k in range(3)]
        ct[3, l] = up[1]
        ct[4, l] = up[2]
        ct[5, l] = down[1]
        ct[6, l] = down[2]
        for n, k in ((7, 0), (8, 2)):
            ct[n, l] = jnp.where(row == 7, pltpu.roll(cfy[1, k, l] * 0.5, 7, 0), pltpu.roll(here[k], 7, 0))
            ct[n + 2, l] = jnp.where(row == 0, pltpu.roll(cfy[0, k, l] * 0.5, 1, 0), pltpu.roll(here[k], 1, 0))
        for n, k in ((11, 0), (12, 1)):
            ct[n, l] = pltpu.roll(here[k], 127, 1)
            ct[n + 2, l] = pltpu.roll(here[k], 1, 1)

    rows = 32

    def fields_of(l):
        coefficients(l)

        def one_row(r, carry):
            c = [jnp.broadcast_to(ct[n, l, pl.ds(r, 1), :], (rows, 128)) for n in range(15)]
            c1, c2, c3, c2xp, c3xp, c2xm, c3xm, c1yp, c3yp, c1ym, c3ym, c1zp, c2zp, c1zm, c2zm = c
            for j in range(128 // rows):
                part = pl.ds(j * rows, rows)
                mid = pad[l + 1, r + 1, part, :].astype(F32)
                xp = pad[l + 2, r + 1, part, :].astype(F32)
                xm = pad[l, r + 1, part, :].astype(F32)
                yp = pad[l + 1, r + 2, part, :].astype(F32)
                ym = pad[l + 1, r, part, :].astype(F32)
                zp = pltpu.roll(mid, 127, 1)
                zm = pltpu.roll(mid, 1, 1)
                g1, g2, g3 = xp - xm, yp - ym, zp - zm
                uv[0, l, r, part, :] = (c2 * g3 - c3 * g2).astype(BF16)
                uv[1, l, r, part, :] = (c3 * g1 - c1 * g3).astype(BF16)
                uv[2, l, r, part, :] = (c1 * g2 - c2 * g1).astype(BF16)
                uv[3, l, r, part, :] = ((c3yp * yp - c3ym * ym) - (c2zp * zp - c2zm * zm)).astype(BF16)
                uv[4, l, r, part, :] = ((c1zp * zp - c1zm * zm) - (c3xp * xp - c3xm * xm)).astype(BF16)
                uv[5, l, r, part, :] = ((c2xp * xp - c2xm * xm) - (c1yp * yp - c1ym * ym)).astype(BF16)
            return carry

        lax.fori_loop(0, 8, one_row, 0)

    def add(t, part, first):
        acc[t] = part if first else acc[t] + part

    def three(k, l):
        return jnp.concatenate([wide(uv[k + i, l]) for i in range(3)], axis=0)

    def add_own(l, first):
        part = lax.dot_general(three(0, l), wide(pad[l + 1, ends]), NT, preferred_element_type=F32)
        for k in range(3):
            add(k, part[k * 128 : k * 128 + 128], first)

    def add_far(side, l, first):
        q = wide(far[side, l])
        t = 3 + 6 * side
        part = lax.dot_general(three(0, l), q, NT, preferred_element_type=F32)
        for k in range(3):
            add(t + k, part[k * 128 : k * 128 + 128], first)
        part = lax.dot_general(q, three(3, l), NT, preferred_element_type=F32)
        for k in range(3):
            add(t + 3 + k, part[:, k * 128 : k * 128 + 128], first)

    def send_sums(group, first, count):
        for t in range(first, first + count):
            stage[t] = acc[t].astype(BF16).reshape(2, 4, 16, 128)
        tiles = pl.ds(first, count)
        copies = []
        for o in (2, 1, 3):
            copy = remote(
                stage.at[tiles, :, lax.rem(dy + o, 4)], from_dy.at[o - 1, tiles],
                sum_s.at[group, o - 1], sum_r.at[group, o - 1], at(b, dx, dy + o),
            )
            copy.start()
            copies.append(copy)
        return copies

    def sums(t, x):
        total = acc[t, pl.ds(pl.multiple_of((x * 4 + dy) * 16, 16), 16), :]
        for o in range(3):
            total = total + from_dy[o, t, x].astype(F32)
        return total

    other = 1 - dx
    home = []

    def send_home(copy):
        copy.start()
        home.append(copy)

    def to_partner(group, first):
        for k in range(3):
            half[3 * group + k] = sums(first + k, other)
        send_home(
            remote(
                half.at[pl.ds(3 * group, 3)], from_dx.at[group], home_s.at[group], home_r.at[group], partner
            )
        )

    def to_panel(side, first, landing):
        for x in (0, 1):
            for k in range(3):
                half[9 + 6 * side + 3 * x + k] = sums(first + k, x)
            send_home(
                remote(
                    half.at[pl.ds(9 + 6 * side + 3 * x, 3)], landing.at[dx],
                    home_s.at[3 + 2 * side + x], home_r.at[3 + 2 * side + dx], at(b + side + 1, x, dy),
                )
            )

    def arrived(copies):
        for copy in copies:
            copy.wait_recv()

    arrived(cy_copies + y_copies)
    fields_of(1)
    fields_of(2)

    @pl.when(near == 1)
    def _():
        pl.semaphore_wait(late, 1)
        start_first(is_root)

    even_down = [remote(pad.at[l + 1, ends], far.at[1, l], chain_s.at[l - 1], far_r.at[1, l], at(b - 2, dx, dy)) for l in (1, 2)]
    even_down += [remote(far.at[0, l], far.at[1, l], chain_s.at[l + 1], far_r.at[1, l], at(b - 1, dx, dy)) for l in (1, 2)]
    odd_down = [remote(lent.at[i], far.at[0, 3 * i], chain_s.at[i], far_r.at[0, 3 * i], at(b - 2, dx, dy)) for i in (0, 1)]
    odd_down += [remote(pad.at[3 * i + 1, ends], far.at[1, 3 * i], chain_s.at[i + 2], far_r.at[1, 3 * i], at(b - 2, dx, dy)) for i in (0, 1)]

    @pl.when(core == 0)
    def _():
        even_down[0].start()
        even_down[1].start()
        hand[1].wait_recv()
        even_down[2].start()
        hand[2].wait_recv()
        even_down[3].start()

    @pl.when(core == 1)
    def _():
        for i in (0, 1):
            lend[i].wait_recv()
            odd_down[i].start()
        for i in (2, 3):
            odd_down[i].start()

    add_own(1, True)
    add_own(2, False)
    arrived(cx_copies + x_copies)
    for l in (0, 3):
        fields_of(l)
        add_own(l, False)
    first_sums = send_sums(0, 0, 3)

    places = [1 - core, 2 + core, core, 3 - core]

    def take(side, n):
        l = places[n]
        dst = far.at[1 - side, l]
        pass_on = remote(far.at[side, l], dst, pass_s.at[n % 2], far_r.at[1 - side, l], mate)
        slot = remote(far.at[side, l], far.at[side, l], pass_s.at[n % 2], far_r.at[side, l], mate)
        if side == 0:
            if n < 2:

                @pl.when(core == 1)
                def _():
                    slot.wait_recv()
                    pass_on.start()

            else:
                slot.wait_recv()
        else:
            slot.wait_recv()
            if n < 2:

                @pl.when(core == 0)
                def _():
                    pass_on.start()

        add_far(side, l, n == 0)
        return pass_on

    passed = []
    for n in range(4):
        passed.append(take(0, n))
    one_sums = send_sums(1, 3, 6)
    arrived(first_sums)
    to_partner(0, 0)
    for n in range(3):
        take(1, n)
    arrived(one_sums)
    to_partner(1, 3)
    to_panel(0, 6, from_one)
    take(1, 3)
    two_sums = send_sums(2, 9, 6)

    def waited(side, x, landing):
        copy = remote(
            half.at[pl.ds(9, 3)], landing.at[x], home_s.at[3 + 2 * side + x], home_r.at[3 + 2 * side + x], partner
        )
        copy.wait_recv()

    def own_rows(group, first):
        home[group if group == 0 else (1 if group == 1 else 4)].wait_recv()
        for k in range(3):
            out[k, 2 + group] = (sums(first + k, dx) + from_dx[group, k]) * scale

    own_rows(0, 0)
    own_rows(1, 3)
    for x in (0, 1):
        waited(0, x, from_one)
    for k in range(3):
        out[k, 1] = (from_one[0, k] + from_one[1, k]) * scale
    arrived(two_sums)
    to_partner(2, 9)
    to_panel(1, 12, from_two)
    own_rows(2, 9)
    for x in (0, 1):
        waited(1, x, from_two)
    for k in range(3):
        out[k, 0] = (from_two[0, k] + from_two[1, k]) * scale

    for copy in x_copies + cx_copies + y_copies + cy_copies + first_sums + one_sums + two_sums + home + even_down:
        copy.wait_send()
    for n in (0, 1):
        passed[n].wait_send()

    @pl.when(core == 0)
    def _():
        for copy in lend:
            copy.wait_send()

    @pl.when(core == 1)
    def _():
        for copy in hand:
            copy.wait_send()


def on_device(n_blk, scale, orbitals, coupling, pot_grad):
    dma = pltpu.SemaphoreType.DMA
    vmem = pl.BlockSpec(memory_space=pltpu.VMEM)
    return pl.pallas_call(
        functools.partial(kernel, n_blk, scale),
        out_shape=jax.ShapeDtypeStruct((3, 5, 16, 128), F32),
        in_specs=[vmem, vmem, vmem],
        out_specs=vmem,
        scratch_shapes=[
            pltpu.VMEM((4096, 128), F32),
            pltpu.VMEM((6, 10, 128, 128), BF16),
            pltpu.VMEM((3, 4, 8, 128), F32),
            pltpu.VMEM((3, 2, 8, 128), F32),
            pltpu.VMEM((2, 3, 4, 8, 128), F32),
            pltpu.VMEM((15, 4, 8, 128), F32),
            pltpu.VMEM((6, 4, 8, 128, 128), BF16),
            pltpu.VMEM((2, 4, 8, 128, 128), BF16),
            pltpu.VMEM((2, 8, 128, 128), BF16),
            pltpu.VMEM((15, 128, 128), F32),
            pltpu.VMEM((15, 2, 4, 16, 128), BF16),
            pltpu.VMEM((3, 15, 2, 16, 128), BF16),
            pltpu.VMEM((21, 16, 128), F32),
            pltpu.VMEM((3, 3, 16, 128), F32),
            pltpu.VMEM((2, 3, 16, 128), F32),
            pltpu.VMEM((2, 3, 16, 128), F32),
            dma((2,)), dma((2,)), dma((2,)), dma((2,)), dma((2,)), dma((2,)), dma((2,)), dma((2,)),
            dma((4,)), dma((2,)), dma((2,)), dma((4,)), dma((2,)), dma((2, 4)),
            dma((3, 3)), dma((3, 3)), dma((7,)), dma((7,)), pltpu.SemaphoreType.REGULAR,
        ],
        compiler_params=pltpu.CompilerParams(
            collective_id=0, has_side_effects=True, vmem_limit_bytes=32 * 1024 * 1024
        ),
    )(orbitals, coupling, pot_grad)


def solution(mesh):
    cells = 8 * 32 * 128
    in_specs = (P("blk", "dx", "dy", None), P("dx", "dy", None), P(None, "dx", "dy", None))
    out_specs = P(None, None, ("blk", "dx", "dy"), None)
    return jax.shard_map(
        functools.partial(on_device, mesh.shape["blk"], 1.0 / math.sqrt(cells)),
        mesh=mesh, in_specs=in_specs, out_specs=out_specs, check_vma=False,
    )
```

```python
import functools
import math

import jax
import jax.numpy as jnp
from jax import lax
from jax.experimental import pallas as pl
from jax.experimental.pallas import tpu as pltpu
from jax.sharding import PartitionSpec as P

MESH = pl.DeviceIdType.MESH
BF16 = jnp.bfloat16
F32 = jnp.float32
NT = (((1,), (1,)), ((), ()))


def wide(value):
    return jnp.concatenate([value[r] for r in range(value.shape[0])], axis=1)


def kernel(
    n_blk, scale,
    psi_in, coupling_in, pot_grad_in, out,
    psi, coupling, pot_grad, flat, pad, cf, cfx, cfy, ct, uv, far, lent, acc, stage, from_dy, half, from_dx, from_one, from_two,
    load_sem, xs, xr, ys, yr, cxs, cxr, cys, cyr, hand_s, lend_s, lend_r, chain_s, pass_s, far_r,
    sum_s, sum_r, home_s, home_r, late,
):
    b, dx, dy = lax.axis_index("blk"), lax.axis_index("dx"), lax.axis_index("dy")
    core = lax.rem(b, 2)

    def at(block, x, y):
        return (lax.rem(block + n_blk, n_blk), x, lax.rem(y + 4, 4))

    def is_root(device):
        return (device[0] == 0) & (device[1] == 0) & (device[2] == 0)

    partner = at(b, 1 - dx, dy)
    mate = at(b + 1 - 2 * core, dx, dy)
    above, below = at(b, dx, dy + 1), at(b, dx, dy - 1)

    def remote(src, dst, send, recv, device):
        return pltpu.make_async_remote_copy(
            src_ref=src, dst_ref=dst, send_sem=send, recv_sem=recv, device_id=device, device_id_type=MESH
        )

    loads = [
        pltpu.make_async_copy(src, dst, load_sem.at[i])
        for i, (src, dst) in enumerate(((psi_in, psi), (coupling_in, coupling), (pot_grad_in, pot_grad)))
    ]
    for load in loads:
        load.start()

    friends = [partner] + [at(b, dx, dy + o) for o in (1, 2, 3)]
    friends += [at(b + d, x, dy) for d in (-2, -1, 1, 2) for x in (0, 1)]
    root = is_root((b, dx, dy))
    near = jnp.int32(0)
    for device in friends:
        near = near + is_root(device).astype(jnp.int32)
    barrier = pltpu.get_barrier_semaphore()

    @pl.when(jnp.logical_not(root))
    def _():
        for device in friends:
            pl.semaphore_signal(barrier, inc=1, device_id=device, device_id_type=MESH)

    for load in loads:
        load.wait()
    for k in range(3):
        cf[k] = coupling[...] * pot_grad[k]

    for j in range(8):
        flat[pl.ds(j * 512, 512), :] = psi[pl.ds(j * 16, 16)].astype(F32).reshape(512, 128)
    for l in range(4):

        def turn(r, carry, l=l):
            pad[l, r + 1] = flat[pl.ds(l * 8 + r, 128, stride=32), :].astype(BF16)
            return carry

        lax.fori_loop(0, 8, turn, 0)
    pl.semaphore_wait(barrier, len(friends) - near)

    @pl.when(root)
    def _():
        for device in friends:
            pl.semaphore_signal(late, inc=1, device_id=device, device_id_type=MESH)

    ends = pl.ds(1, 8)
    layers = pl.ds(0, 4)
    x_copies = [remote(pad.at[0, ends], pad.at[4, ends], xs, xr, partner)]
    cx_copies = [remote(cf.at[:, 0], cfx, cxs, cxr, partner)]
    y_copies = [
        remote(pad.at[layers, 8], pad.at[layers, 0], ys.at[0], yr.at[0], above),
        remote(pad.at[layers, 1], pad.at[layers, 9], ys.at[1], yr.at[1], below),
    ]
    cy_copies = [
        remote(cf, cfy.at[0], cys.at[0], cyr.at[0], above),
        remote(cf, cfy.at[1], cys.at[1], cyr.at[1], below),
    ]
    hand = [remote(pad.at[l, ends], far.at[0, l], hand_s.at[l], far_r.at[0, l], mate) for l in range(5)]
    lend = [remote(pad.at[3 * i, ends], lent.at[i], lend_s.at[i], lend_r.at[i], mate) for i in range(2)]

    chip_before = at(b - 2, dx, dy)

    def down(src, side, l, n, device):
        return remote(src, far.at[side, l], chain_s.at[n], far_r.at[side, l], device)

    even_down = [down(pad.at[l, ends], 1, l, n, chip_before) for n, l in enumerate((1, 2, 4))]
    even_down += [down(far.at[0, l], 1, l, 2 + l, at(b - 1, dx, dy)) for l in (1, 2)]
    odd_down = [down(lent.at[i], 0, 3 * i, i, chip_before) for i in (0, 1)]
    odd_down += [down(pad.at[l, ends], 1, l, n, chip_before) for n, l in ((2, 0), (3, 3), (4, 4))]

    def start_first(when):
        groups = [
            (partner, cx_copies + x_copies),
            (above, [cy_copies[0], y_copies[0]]),
            (below, [cy_copies[1], y_copies[1]]),
        ]
        for device, copies in groups:

            @pl.when(when(device))
            def _(copies=copies):
                for copy in copies:
                    copy.start()

        @pl.when(when(mate) & (core == 1))
        def _():
            for l in (1, 2, 0, 3):
                hand[l].start()

        @pl.when(when(mate) & (core == 0))
        def _():
            for copy in lend:
                copy.start()

        @pl.when(when(chip_before) & (core == 0))
        def _():
            even_down[0].start()
            even_down[1].start()

    start_first(lambda device: jnp.logical_not(is_root(device)))

    row = lax.broadcasted_iota(jnp.int32, (8, 128), 0)

    def coefficients(l):
        here = [cf[k, l] * 0.5 for k in range(3)]
        for k in range(3):
            ct[k, l] = here[k]
        for n, k in ((3, 1), (4, 2)):
            ct[n, l] = (cf[k, l + 1] if l < 3 else cfx[k]) * 0.5
            if l > 0:
                ct[n + 2, l] = cf[k, l - 1] * 0.5
        for n, k in ((7, 0), (8, 2)):
            ct[n, l] = jnp.where(row == 7, pltpu.roll(cfy[1, k, l] * 0.5, 7, 0), pltpu.roll(here[k], 7, 0))
            ct[n + 2, l] = jnp.where(row == 0, pltpu.roll(cfy[0, k, l] * 0.5, 1, 0), pltpu.roll(here[k], 1, 0))
        for n, k in ((11, 0), (12, 1)):
            ct[n, l] = pltpu.roll(here[k], 127, 1)
            ct[n + 2, l] = pltpu.roll(here[k], 1, 1)

    rows = 32

    def fields_of(l):
        coefficients(l)

        def one_row(r, carry):
            c = [None if l == 0 and n in (5, 6) else jnp.broadcast_to(ct[n, l, pl.ds(r, 1), :], (rows, 128)) for n in range(15)]
            c1, c2, c3, c2xp, c3xp, c2xm, c3xm, c1yp, c3yp, c1ym, c3ym, c1zp, c2zp, c1zm, c2zm = c
            for j in range(128 // rows):
                part = pl.ds(j * rows, rows)
                mid = pad[l, r + 1, part, :].astype(F32)
                xp = pad[l + 1, r + 1, part, :].astype(F32)
                yp = pad[l, r + 2, part, :].astype(F32)
                ym = pad[l, r, part, :].astype(F32)
                zp = pltpu.roll(mid, 127, 1)
                zm = pltpu.roll(mid, 1, 1)
                g1, g2, g3 = xp, yp - ym, zp - zm
                c2x, c3x = c2xp * xp, c3xp * xp
                if l > 0:
                    xm = pad[l - 1, r + 1, part, :].astype(F32)
                    g1, c2x, c3x = g1 - xm, c2x - c2xm * xm, c3x - c3xm * xm
                uv[0, l, r, part, :] = (c2 * g3 - c3 * g2).astype(BF16)
                uv[1, l, r, part, :] = (c3 * g1 - c1 * g3).astype(BF16)
                uv[2, l, r, part, :] = (c1 * g2 - c2 * g1).astype(BF16)
                uv[3, l, r, part, :] = ((c3yp * yp - c3ym * ym) - (c2zp * zp - c2zm * zm)).astype(BF16)
                uv[4, l, r, part, :] = ((c1zp * zp - c1zm * zm) - c3x).astype(BF16)
                uv[5, l, r, part, :] = (c2x - (c1yp * yp - c1ym * ym)).astype(BF16)
            return carry

        lax.fori_loop(0, 8, one_row, 0)

    def fields_at_the_end():
        for n, k in ((0, 1), (1, 2)):
            ct[n, 4] = cfx[k] * 0.5

        def one_row(r, carry):
            c2, c3 = [jnp.broadcast_to(ct[n, 4, pl.ds(r, 1), :], (128, 128)) for n in (0, 1)]
            c2xm, c3xm = [jnp.broadcast_to(ct[n, 3, pl.ds(r, 1), :], (128, 128)) for n in (1, 2)]
            xm = pad[3, r + 1].astype(F32)
            uv[1, 4, r] = (-(c3 * xm)).astype(BF16)
            uv[2, 4, r] = (c2 * xm).astype(BF16)
            uv[4, 4, r] = (c3xm * xm).astype(BF16)
            uv[5, 4, r] = (-(c2xm * xm)).astype(BF16)
            return carry

        lax.fori_loop(0, 8, one_row, 0)

    def add(t, part, first):
        acc[t] = part if first else acc[t] + part

    def fields(k, l, end):
        return jnp.concatenate([wide(uv[k + i, l]) for i in range(1 if end else 0, 3)], axis=0)

    def add_own(l, first, end=False):
        part = lax.dot_general(fields(0, l, end), wide(pad[l, ends]), NT, preferred_element_type=F32)
        for i, k in enumerate((1, 2) if end else (0, 1, 2)):
            add(k, part[i * 128 : i * 128 + 128], first)

    def add_far(side, l, first, end=False):
        q = wide(far[side, l])
        t = 3 + 6 * side
        part = lax.dot_general(fields(0, l, end), q, NT, preferred_element_type=F32)
        back = lax.dot_general(q, fields(3, l, end), NT, preferred_element_type=F32)
        for i, k in enumerate((1, 2) if end else (0, 1, 2)):
            add(t + k, part[i * 128 : i * 128 + 128], first)
            add(t + 3 + k, back[:, i * 128 : i * 128 + 128], first)

    def send_sums(group, first, count):
        for t in range(first, first + count):
            stage[t] = acc[t].astype(BF16).reshape(2, 4, 16, 128)
        tiles = pl.ds(first, count)
        copies = []
        for o in (2, 1, 3):
            copy = remote(
                stage.at[tiles, :, lax.rem(dy + o, 4)], from_dy.at[o - 1, tiles],
                sum_s.at[group, o - 1], sum_r.at[group, o - 1], at(b, dx, dy + o),
            )
            copy.start()
            copies.append(copy)
        return copies

    def sums(t, x):
        total = acc[t, pl.ds(pl.multiple_of((x * 4 + dy) * 16, 16), 16), :]
        for o in range(3):
            total = total + from_dy[o, t, x].astype(F32)
        return total

    other = 1 - dx
    home = []

    def send_home(copy):
        copy.start()
        home.append(copy)

    def to_partner(group, first):
        for k in range(3):
            half[3 * group + k] = sums(first + k, other)
        send_home(
            remote(
                half.at[pl.ds(3 * group, 3)], from_dx.at[group], home_s.at[group], home_r.at[group], partner
            )
        )

    def to_panel(side, first, landing):
        for x in (0, 1):
            for k in range(3):
                half[9 + 6 * side + 3 * x + k] = sums(first + k, x)
            send_home(
                remote(
                    half.at[pl.ds(9 + 6 * side + 3 * x, 3)], landing.at[dx],
                    home_s.at[3 + 2 * side + x], home_r.at[3 + 2 * side + dx], at(b + side + 1, x, dy),
                )
            )

    def arrived(copies):
        for copy in copies:
            copy.wait_recv()

    arrived(cy_copies + y_copies)
    fields_of(0)

    @pl.when(core == 1)
    def _():
        for i in (0, 1):
            lend[i].wait_recv()
            odd_down[i].start()
        odd_down[2].start()
        odd_down[3].start()

    fields_of(1)
    fields_of(2)

    @pl.when(near == 1)
    def _():
        pl.semaphore_wait(late, 1)
        start_first(is_root)

    for l in range(3):
        add_own(l, l == 0)
    arrived(cx_copies + x_copies)

    @pl.when(core == 0)
    def _():
        even_down[2].start()
        for l in (1, 2):
            hand[l].wait_recv()
            even_down[2 + l].start()

    @pl.when(core == 1)
    def _():
        odd_down[4].start()
        hand[4].start()

    fields_of(3)
    fields_at_the_end()
    add_own(3, False)
    add_own(4, False, True)
    first_sums = send_sums(0, 0, 3)

    places = [1 - core, 2 + core, core, 3 - core, 4]

    def take(side, n):
        l = places[n]
        pass_on = remote(
            far.at[side, l], far.at[1 - side, l], pass_s.at[min(n, 2) if n != 4 else 2], far_r.at[1 - side, l], mate
        )
        slot = remote(far.at[side, l], far.at[side, l], pass_s.at[0], far_r.at[side, l], mate)
        if side == 0:
            if n < 2:

                @pl.when(core == 1)
                def _():
                    slot.wait_recv()
                    pass_on.start()

            else:
                slot.wait_recv()
        else:
            slot.wait_recv()
            if n in (0, 1, 4):

                @pl.when(core == 0)
                def _():
                    pass_on.start()

        add_far(side, l, n == 0, n == 4)
        return pass_on

    passed = []
    for n in range(5):
        passed.append(take(0, n))
    one_sums = send_sums(1, 3, 6)
    arrived(first_sums)
    to_partner(0, 0)
    for n in range(4):
        take(1, n)
    arrived(one_sums)
    to_partner(1, 3)
    to_panel(0, 6, from_one)
    take(1, 4)
    two_sums = send_sums(2, 9, 6)

    def waited(side, x, landing):
        copy = remote(
            half.at[pl.ds(9, 3)], landing.at[x], home_s.at[3 + 2 * side + x], home_r.at[3 + 2 * side + x], partner
        )
        copy.wait_recv()

    def own_rows(group, first):
        home[group if group == 0 else (1 if group == 1 else 4)].wait_recv()
        for k in range(3):
            out[k, 2 + group] = (sums(first + k, dx) + from_dx[group, k]) * scale

    own_rows(0, 0)
    own_rows(1, 3)
    for x in (0, 1):
        waited(0, x, from_one)
    for k in range(3):
        out[k, 1] = (from_one[0, k] + from_one[1, k]) * scale
    arrived(two_sums)
    to_partner(2, 9)
    to_panel(1, 12, from_two)
    own_rows(2, 9)
    for x in (0, 1):
        waited(1, x, from_two)
    for k in range(3):
        out[k, 0] = (from_two[0, k] + from_two[1, k]) * scale

    for copy in x_copies + cx_copies + y_copies + cy_copies + first_sums + one_sums + two_sums + home + even_down:
        copy.wait_send()
    for n in (0, 1):
        passed[n].wait_send()

    @pl.when(core == 0)
    def _():
        passed[4].wait_send()
        for copy in lend:
            copy.wait_send()

    @pl.when(core == 1)
    def _():
        for copy in hand:
            copy.wait_send()


def on_device(n_blk, scale, orbitals, coupling, pot_grad):
    dma = pltpu.SemaphoreType.DMA
    vmem = pl.BlockSpec(memory_space=pltpu.VMEM)
    return pl.pallas_call(
        functools.partial(kernel, n_blk, scale),
        out_shape=jax.ShapeDtypeStruct((3, 5, 16, 128), F32),
        in_specs=[pl.BlockSpec(memory_space=pltpu.HBM)] * 3,
        out_specs=vmem,
        scratch_shapes=[
            pltpu.VMEM((128, 4, 8, 128), BF16),
            pltpu.VMEM((4, 8, 128), F32),
            pltpu.VMEM((3, 4, 8, 128), F32),
            pltpu.VMEM((4096, 128), F32),
            pltpu.VMEM((5, 10, 128, 128), BF16),
            pltpu.VMEM((3, 4, 8, 128), F32),
            pltpu.VMEM((3, 8, 128), F32),
            pltpu.VMEM((2, 3, 4, 8, 128), F32),
            pltpu.VMEM((15, 5, 8, 128), F32),
            pltpu.VMEM((6, 5, 8, 128, 128), BF16),
            pltpu.VMEM((2, 5, 8, 128, 128), BF16),
            pltpu.VMEM((2, 8, 128, 128), BF16),
            pltpu.VMEM((15, 128, 128), F32),
            pltpu.VMEM((15, 2, 4, 16, 128), BF16),
            pltpu.VMEM((3, 15, 2, 16, 128), BF16),
            pltpu.VMEM((21, 16, 128), F32),
            pltpu.VMEM((3, 3, 16, 128), F32),
            pltpu.VMEM((2, 3, 16, 128), F32),
            pltpu.VMEM((2, 3, 16, 128), F32),
            dma((3,)), dma, dma, dma((2,)), dma((2,)), dma, dma, dma((2,)), dma((2,)),
            dma((5,)), dma((2,)), dma((2,)), dma((5,)), dma((3,)), dma((2, 5)),
            dma((3, 3)), dma((3, 3)), dma((7,)), dma((7,)), pltpu.SemaphoreType.REGULAR,
        ],
        compiler_params=pltpu.CompilerParams(
            collective_id=0, has_side_effects=True, vmem_limit_bytes=67043328 - 128 * 1024
        ),
    )(orbitals, coupling, pot_grad)


def solution(mesh):
    cells = 8 * 32 * 128
    in_specs = (P("blk", "dx", "dy", None), P("dx", "dy", None), P(None, "dx", "dy", None))
    out_specs = P(None, None, ("blk", "dx", "dy"), None)
    return jax.shard_map(
        functools.partial(on_device, mesh.shape["blk"], 1.0 / math.sqrt(cells)),
        mesh=mesh, in_specs=in_specs, out_specs=out_specs, check_vma=False,
    )
```

```python
import functools
import math

import jax
import jax.numpy as jnp
from jax import lax
from jax.experimental import pallas as pl
from jax.experimental.pallas import tpu as pltpu
from jax.sharding import PartitionSpec as P

MESH = pl.DeviceIdType.MESH
BF16 = jnp.bfloat16
F32 = jnp.float32
NT = (((1,), (1,)), ((), ()))


def wide(value):
    return jnp.concatenate([value[r] for r in range(value.shape[0])], axis=1)


def kernel(
    n_blk, scale,
    psi_in, coupling_in, pot_grad_in, out,
    psi, coupling, pot_grad, flat, pad, cf, cfx, cfy, ct, uv, far, lent, acc, stage, from_dy, half, from_dx, from_one, from_two,
    load_sem, xs, xr, ys, yr, cxs, cxr, cys, cyr, hand_s, lend_s, lend_r, chain_s, pass_s, far_r,
    sum_s, sum_r, home_s, home_r, late,
):
    b, dx, dy = lax.axis_index("blk"), lax.axis_index("dx"), lax.axis_index("dy")
    core = lax.rem(b, 2)

    def at(block, x, y):
        return (lax.rem(block + n_blk, n_blk), x, lax.rem(y + 4, 4))

    def is_root(device):
        return (device[0] == 0) & (device[1] == 0) & (device[2] == 0)

    partner = at(b, 1 - dx, dy)
    mate = at(b + 1 - 2 * core, dx, dy)
    above, below = at(b, dx, dy + 1), at(b, dx, dy - 1)

    def remote(src, dst, send, recv, device):
        return pltpu.make_async_remote_copy(
            src_ref=src, dst_ref=dst, send_sem=send, recv_sem=recv, device_id=device, device_id_type=MESH
        )

    loads = [
        pltpu.make_async_copy(src, dst, load_sem.at[i])
        for i, (src, dst) in enumerate(((psi_in, psi), (coupling_in, coupling), (pot_grad_in, pot_grad)))
    ]
    for load in loads:
        load.start()

    friends = [partner] + [at(b, dx, dy + o) for o in (1, 2, 3)]
    friends += [at(b + d, x, dy) for d in (-2, -1, 1, 2) for x in (0, 1)]
    root = is_root((b, dx, dy))
    near = jnp.int32(0)
    for device in friends:
        near = near + is_root(device).astype(jnp.int32)
    barrier = pltpu.get_barrier_semaphore()

    @pl.when(jnp.logical_not(root))
    def _():
        for device in friends:
            pl.semaphore_signal(barrier, inc=1, device_id=device, device_id_type=MESH)

    for load in loads:
        load.wait()
    for k in range(3):
        cf[k] = coupling[...] * pot_grad[k]

    for j in range(8):
        flat[pl.ds(j * 512, 512), :] = psi[pl.ds(j * 16, 16)].astype(F32).reshape(512, 128)
    for l in range(4):

        def turn(r, carry, l=l):
            pad[l, r + 1] = flat[pl.ds(l * 8 + r, 128, stride=32), :].astype(BF16)
            return carry

        lax.fori_loop(0, 8, turn, 0)
    pl.semaphore_wait(barrier, len(friends) - near)

    @pl.when(root)
    def _():
        for device in friends:
            pl.semaphore_signal(late, inc=1, device_id=device, device_id_type=MESH)

    ends = pl.ds(1, 8)
    layers = pl.ds(0, 4)
    x_copies = [remote(pad.at[0, ends], pad.at[4, ends], xs, xr, partner)]
    cx_copies = [remote(cf.at[:, 0], cfx, cxs, cxr, partner)]
    y_copies = [
        remote(pad.at[layers, 8], pad.at[layers, 0], ys.at[0], yr.at[0], above),
        remote(pad.at[layers, 1], pad.at[layers, 9], ys.at[1], yr.at[1], below),
    ]
    cy_copies = [
        remote(cf, cfy.at[0], cys.at[0], cyr.at[0], above),
        remote(cf, cfy.at[1], cys.at[1], cyr.at[1], below),
    ]
    hand = [remote(pad.at[l, ends], far.at[0, l], hand_s.at[l], far_r.at[0, l], mate) for l in range(5)]
    lend = [remote(pad.at[3 * i, ends], lent.at[i], lend_s.at[i], lend_r.at[i], mate) for i in range(2)]

    chip_before = at(b - 2, dx, dy)

    def down(src, side, l, n, device):
        return remote(src, far.at[side, l], chain_s.at[n], far_r.at[side, l], device)

    even_down = [down(pad.at[l, ends], 1, l, n, chip_before) for n, l in enumerate((1, 2, 4))]
    even_down += [down(far.at[0, l], 1, l, 2 + l, at(b - 1, dx, dy)) for l in (1, 2)]
    odd_down = [down(lent.at[i], 0, 3 * i, i, chip_before) for i in (0, 1)]
    odd_down += [down(pad.at[l, ends], 1, l, n, chip_before) for n, l in ((2, 0), (3, 3), (4, 4))]

    def start_first(when):
        groups = [
            (partner, cx_copies + x_copies),
            (above, [cy_copies[0], y_copies[0]]),
            (below, [cy_copies[1], y_copies[1]]),
        ]
        for device, copies in groups:

            @pl.when(when(device))
            def _(copies=copies):
                for copy in copies:
                    copy.start()

        @pl.when(when(mate) & (core == 1))
        def _():
            for l in (1, 2, 0, 3):
                hand[l].start()

        @pl.when(when(mate) & (core == 0))
        def _():
            for copy in lend:
                copy.start()

        @pl.when(when(chip_before) & (core == 0))
        def _():
            even_down[0].start()
            even_down[1].start()

    start_first(lambda device: jnp.logical_not(is_root(device)))

    row = lax.broadcasted_iota(jnp.int32, (8, 128), 0)

    def coefficients(l):
        here = [cf[k, l] * 0.5 for k in range(3)]
        for k in range(3):
            ct[k, l] = here[k]
        for n, k in ((3, 1), (4, 2)):
            ct[n, l] = (cf[k, l + 1] if l < 3 else cfx[k]) * 0.5
            if l > 0:
                ct[n + 2, l] = cf[k, l - 1] * 0.5
        for n, k in ((7, 0), (8, 2)):
            ct[n, l] = jnp.where(row == 7, pltpu.roll(cfy[1, k, l] * 0.5, 7, 0), pltpu.roll(here[k], 7, 0))
            ct[n + 2, l] = jnp.where(row == 0, pltpu.roll(cfy[0, k, l] * 0.5, 1, 0), pltpu.roll(here[k], 1, 0))
        for n, k in ((11, 0), (12, 1)):
            ct[n, l] = pltpu.roll(here[k], 127, 1)
            ct[n + 2, l] = pltpu.roll(here[k], 1, 1)

    rows = 32

    def fields_of(l):
        coefficients(l)

        def one_row(r, carry):
            c = [None if l == 0 and n in (5, 6) else jnp.broadcast_to(ct[n, l, pl.ds(r, 1), :], (rows, 128)) for n in range(15)]
            c1, c2, c3, c2xp, c3xp, c2xm, c3xm, c1yp, c3yp, c1ym, c3ym, c1zp, c2zp, c1zm, c2zm = c
            for j in range(128 // rows):
                part = pl.ds(j * rows, rows)
                mid = pad[l, r + 1, part, :].astype(F32)
                xp = pad[l + 1, r + 1, part, :].astype(F32)
                yp = pad[l, r + 2, part, :].astype(F32)
                ym = pad[l, r, part, :].astype(F32)
                zp = pltpu.roll(mid, 127, 1)
                zm = pltpu.roll(mid, 1, 1)
                g1, g2, g3 = xp, yp - ym, zp - zm
                c2x, c3x = c2xp * xp, c3xp * xp
                if l > 0:
                    xm = pad[l - 1, r + 1, part, :].astype(F32)
                    g1, c2x, c3x = g1 - xm, c2x - c2xm * xm, c3x - c3xm * xm
                uv[0, l, r, part, :] = (c2 * g3 - c3 * g2).astype(BF16)
                uv[1, l, r, part, :] = (c3 * g1 - c1 * g3).astype(BF16)
                uv[2, l, r, part, :] = (c1 * g2 - c2 * g1).astype(BF16)
                uv[3, l, r, part, :] = ((c3yp * yp - c3ym * ym) - (c2zp * zp - c2zm * zm)).astype(BF16)
                uv[4, l, r, part, :] = ((c1zp * zp - c1zm * zm) - c3x).astype(BF16)
                uv[5, l, r, part, :] = (c2x - (c1yp * yp - c1ym * ym)).astype(BF16)
            return carry

        lax.fori_loop(0, 8, one_row, 0)

    def fields_at_the_end():
        for n, k in ((0, 1), (1, 2)):
            ct[n, 4] = cfx[k] * 0.5

        def one_row(r, carry):
            c2, c3 = [jnp.broadcast_to(ct[n, 4, pl.ds(r, 1), :], (128, 128)) for n in (0, 1)]
            c2xm, c3xm = [jnp.broadcast_to(ct[n, 3, pl.ds(r, 1), :], (128, 128)) for n in (1, 2)]
            xm = pad[3, r + 1].astype(F32)
            uv[1, 4, r] = (-(c3 * xm)).astype(BF16)
            uv[2, 4, r] = (c2 * xm).astype(BF16)
            uv[4, 4, r] = (c3xm * xm).astype(BF16)
            uv[5, 4, r] = (-(c2xm * xm)).astype(BF16)
            return carry

        lax.fori_loop(0, 8, one_row, 0)

    def add(t, part, first):
        acc[t] = part if first else acc[t] + part

    def fields(k, l, end):
        return jnp.concatenate([wide(uv[k + i, l]) for i in range(1 if end else 0, 3)], axis=0)

    def add_own(l, first, end=False):
        part = lax.dot_general(fields(0, l, end), wide(pad[l, ends]), NT, preferred_element_type=F32)
        for i, k in enumerate((1, 2) if end else (0, 1, 2)):
            add(k, part[i * 128 : i * 128 + 128], first)

    def add_back(side, l, first, end=False):
        back = lax.dot_general(wide(far[side, l]), fields(3, l, end), NT, preferred_element_type=F32)
        for i, k in enumerate((1, 2) if end else (0, 1, 2)):
            add(6 + 6 * side + k, back[:, i * 128 : i * 128 + 128], first)

    def add_far(side, l, first, end=False):
        part = lax.dot_general(fields(0, l, end), wide(far[side, l]), NT, preferred_element_type=F32)
        for i, k in enumerate((1, 2) if end else (0, 1, 2)):
            add(3 + 6 * side + k, part[i * 128 : i * 128 + 128], first)

    def send_sums(group, first, count):
        for t in range(first, first + count):
            stage[t] = acc[t].astype(BF16).reshape(2, 4, 16, 128)
        tiles = pl.ds(first, count)
        copies = []
        for o in (2, 1, 3):
            copy = remote(
                stage.at[tiles, :, lax.rem(dy + o, 4)], from_dy.at[o - 1, tiles],
                sum_s.at[group, o - 1], sum_r.at[group, o - 1], at(b, dx, dy + o),
            )
            copy.start()
            copies.append(copy)
        return copies

    def sums(t, x):
        total = acc[t, pl.ds(pl.multiple_of((x * 4 + dy) * 16, 16), 16), :]
        for o in range(3):
            total = total + from_dy[o, t, x].astype(F32)
        return total

    other = 1 - dx
    home = []

    def send_home(copy):
        copy.start()
        home.append(copy)

    def to_partner(group, first):
        for k in range(3):
            half[3 * group + k] = sums(first + k, other)
        send_home(
            remote(
                half.at[pl.ds(3 * group, 3)], from_dx.at[group], home_s.at[group], home_r.at[group], partner
            )
        )

    def to_panel(side, first, landing):
        for x in (0, 1):
            for k in range(3):
                half[9 + 6 * side + 3 * x + k] = sums(first + k, x)
            send_home(
                remote(
                    half.at[pl.ds(9 + 6 * side + 3 * x, 3)], landing.at[dx],
                    home_s.at[3 + 2 * side + x], home_r.at[3 + 2 * side + dx], at(b + side + 1, x, dy),
                )
            )

    def arrived(copies):
        for copy in copies:
            copy.wait_recv()

    arrived(cy_copies + y_copies)
    fields_of(0)

    @pl.when(core == 1)
    def _():
        for i in (0, 1):
            lend[i].wait_recv()
            odd_down[i].start()
        odd_down[2].start()
        odd_down[3].start()

    fields_of(1)
    fields_of(2)

    @pl.when(near == 1)
    def _():
        pl.semaphore_wait(late, 1)
        start_first(is_root)

    for l in range(3):
        add_own(l, l == 0)
    arrived(cx_copies + x_copies)

    @pl.when(core == 0)
    def _():
        even_down[2].start()
        for l in (1, 2):
            hand[l].wait_recv()
            even_down[2 + l].start()

    @pl.when(core == 1)
    def _():
        odd_down[4].start()
        hand[4].start()

    fields_of(3)
    fields_at_the_end()
    add_own(3, False)
    add_own(4, False, True)
    first_sums = send_sums(0, 0, 3)

    places = [1 - core, 2 + core, core, 3 - core, 4]

    def take(side, n):
        l = places[n]
        pass_on = remote(
            far.at[side, l], far.at[1 - side, l], pass_s.at[min(n, 2) if n != 4 else 2], far_r.at[1 - side, l], mate
        )
        slot = remote(far.at[side, l], far.at[side, l], pass_s.at[0], far_r.at[side, l], mate)
        if side == 0:
            if n < 2:

                @pl.when(core == 1)
                def _():
                    slot.wait_recv()
                    pass_on.start()

            else:
                slot.wait_recv()
        else:
            slot.wait_recv()
            if n in (0, 1, 4):

                @pl.when(core == 0)
                def _():
                    pass_on.start()

        add_back(side, l, n == 0, n == 4)
        if side == 0 or n < 4:
            add_far(side, l, n == 0, n == 4)
        return pass_on

    passed = []
    for n in range(5):
        passed.append(take(0, n))
    one_sums = send_sums(1, 3, 6)
    arrived(first_sums)
    to_partner(0, 0)
    for n in range(4):
        take(1, n)
    arrived(one_sums)
    to_partner(1, 3)
    to_panel(0, 6, from_one)
    take(1, 4)
    back_sums = send_sums(2, 12, 3)
    add_far(1, 4, False, True)
    two_sums = send_sums(3, 9, 3)
    arrived(back_sums)
    to_panel(1, 12, from_two)
    arrived(two_sums)
    to_partner(2, 9)

    def waited(side, x, landing):
        copy = remote(
            half.at[pl.ds(9, 3)], landing.at[x], home_s.at[3 + 2 * side + x], home_r.at[3 + 2 * side + x], partner
        )
        copy.wait_recv()

    def own_rows(group, first):
        home[(0, 1, 6)[group]].wait_recv()
        for k in range(3):
            out[k, 2 + group] = (sums(first + k, dx) + from_dx[group, k]) * scale

    own_rows(0, 0)
    own_rows(1, 3)
    for x in (0, 1):
        waited(0, x, from_one)
    for k in range(3):
        out[k, 1] = (from_one[0, k] + from_one[1, k]) * scale
    own_rows(2, 9)
    for x in (0, 1):
        waited(1, x, from_two)
    for k in range(3):
        out[k, 0] = (from_two[0, k] + from_two[1, k]) * scale

    for copy in x_copies + cx_copies + y_copies + cy_copies + first_sums + one_sums + back_sums + two_sums + home + even_down:
        copy.wait_send()
    for n in (0, 1):
        passed[n].wait_send()

    @pl.when(core == 0)
    def _():
        passed[4].wait_send()
        for copy in lend:
            copy.wait_send()

    @pl.when(core == 1)
    def _():
        for copy in hand:
            copy.wait_send()


def on_device(n_blk, scale, orbitals, coupling, pot_grad):
    dma = pltpu.SemaphoreType.DMA
    vmem = pl.BlockSpec(memory_space=pltpu.VMEM)
    return pl.pallas_call(
        functools.partial(kernel, n_blk, scale),
        out_shape=jax.ShapeDtypeStruct((3, 5, 16, 128), F32),
        in_specs=[pl.BlockSpec(memory_space=pltpu.HBM)] * 3,
        out_specs=vmem,
        scratch_shapes=[
            pltpu.VMEM((128, 4, 8, 128), BF16),
            pltpu.VMEM((4, 8, 128), F32),
            pltpu.VMEM((3, 4, 8, 128), F32),
            pltpu.VMEM((4096, 128), F32),
            pltpu.VMEM((5, 10, 128, 128), BF16),
            pltpu.VMEM((3, 4, 8, 128), F32),
            pltpu.VMEM((3, 8, 128), F32),
            pltpu.VMEM((2, 3, 4, 8, 128), F32),
            pltpu.VMEM((15, 5, 8, 128), F32),
            pltpu.VMEM((6, 5, 8, 128, 128), BF16),
            pltpu.VMEM((2, 5, 8, 128, 128), BF16),
            pltpu.VMEM((2, 8, 128, 128), BF16),
            pltpu.VMEM((15, 128, 128), F32),
            pltpu.VMEM((15, 2, 4, 16, 128), BF16),
            pltpu.VMEM((3, 15, 2, 16, 128), BF16),
            pltpu.VMEM((21, 16, 128), F32),
            pltpu.VMEM((3, 3, 16, 128), F32),
            pltpu.VMEM((2, 3, 16, 128), F32),
            pltpu.VMEM((2, 3, 16, 128), F32),
            dma((3,)), dma, dma, dma((2,)), dma((2,)), dma, dma, dma((2,)), dma((2,)),
            dma((5,)), dma((2,)), dma((2,)), dma((5,)), dma((3,)), dma((2, 5)),
            dma((4, 3)), dma((4, 3)), dma((7,)), dma((7,)), pltpu.SemaphoreType.REGULAR,
        ],
        compiler_params=pltpu.CompilerParams(
            collective_id=0, has_side_effects=True, vmem_limit_bytes=67043328 - 128 * 1024
        ),
    )(orbitals, coupling, pot_grad)


def solution(mesh):
    cells = 8 * 32 * 128
    in_specs = (P("blk", "dx", "dy", None), P("dx", "dy", None), P(None, "dx", "dy", None))
    out_specs = P(None, None, ("blk", "dx", "dy"), None)
    return jax.shard_map(
        functools.partial(on_device, mesh.shape["blk"], 1.0 / math.sqrt(cells)),
        mesh=mesh, in_specs=in_specs, out_specs=out_specs, check_vma=False,
    )
```

```python
import functools
import math

import jax
import jax.numpy as jnp
from jax import lax
from jax.experimental import pallas as pl
from jax.experimental.pallas import tpu as pltpu
from jax.sharding import PartitionSpec as P

MESH = pl.DeviceIdType.MESH
BF16 = jnp.bfloat16
F32 = jnp.float32
NT = (((1,), (1,)), ((), ()))


def wide(value):
    return jnp.concatenate([value[r] for r in range(value.shape[0])], axis=1)


def kernel(
    n_blk, scale,
    psi_in, coupling_in, pot_grad_in, out,
    psi, coupling, pot_grad, flat, pad, cf, cfx, cfy, ct, uv, far, lent, acc, stage, from_dy, half, from_dx, from_one, from_two,
    load_sem, xs, xr, ys, yr, cxs, cxr, cys, cyr, hand_s, lend_s, lend_r, chain_s, pass_s, far_r,
    sum_s, sum_r, home_s, home_r, late,
):
    b, dx, dy = lax.axis_index("blk"), lax.axis_index("dx"), lax.axis_index("dy")
    core = lax.rem(b, 2)

    def at(block, x, y):
        return (lax.rem(block + n_blk, n_blk), x, lax.rem(y + 4, 4))

    def is_root(device):
        return (device[0] == 0) & (device[1] == 0) & (device[2] == 0)

    partner = at(b, 1 - dx, dy)
    mate = at(b + 1 - 2 * core, dx, dy)
    above, below = at(b, dx, dy + 1), at(b, dx, dy - 1)

    def remote(src, dst, send, recv, device):
        return pltpu.make_async_remote_copy(
            src_ref=src, dst_ref=dst, send_sem=send, recv_sem=recv, device_id=device, device_id_type=MESH
        )

    loads = [
        pltpu.make_async_copy(src, dst, load_sem.at[i])
        for i, (src, dst) in enumerate(((psi_in, psi), (coupling_in, coupling), (pot_grad_in, pot_grad)))
    ]
    for load in loads:
        load.start()

    friends = [partner] + [at(b, dx, dy + o) for o in (1, 2, 3)]
    friends += [at(b + d, x, dy) for d in (-2, -1, 1, 2) for x in (0, 1)]
    root = is_root((b, dx, dy))
    near = jnp.int32(0)
    for device in friends:
        near = near + is_root(device).astype(jnp.int32)
    barrier = pltpu.get_barrier_semaphore()

    @pl.when(jnp.logical_not(root))
    def _():
        for device in friends:
            pl.semaphore_signal(barrier, inc=1, device_id=device, device_id_type=MESH)

    for load in loads:
        load.wait()
    for k in range(3):
        cf[k] = coupling[...] * pot_grad[k]

    for j in range(8):
        flat[pl.ds(j * 512, 512), :] = psi[pl.ds(j * 16, 16)].astype(F32).reshape(512, 128)
    for l in range(4):

        def turn(r, carry, l=l):
            pad[l, r + 1] = flat[pl.ds(l * 8 + r, 128, stride=32), :].astype(BF16)
            return carry

        lax.fori_loop(0, 8, turn, 0)
    pl.semaphore_wait(barrier, len(friends) - near)

    @pl.when(root)
    def _():
        for device in friends:
            pl.semaphore_signal(late, inc=1, device_id=device, device_id_type=MESH)

    ends = pl.ds(1, 8)
    layers = pl.ds(0, 4)
    x_copies = [remote(pad.at[0, ends], pad.at[4, ends], xs, xr, partner)]
    cx_copies = [remote(cf.at[:, 0], cfx, cxs, cxr, partner)]
    y_copies = [
        remote(pad.at[layers, 8], pad.at[layers, 0], ys.at[0], yr.at[0], above),
        remote(pad.at[layers, 1], pad.at[layers, 9], ys.at[1], yr.at[1], below),
    ]
    cy_copies = [
        remote(cf, cfy.at[0], cys.at[0], cyr.at[0], above),
        remote(cf, cfy.at[1], cys.at[1], cyr.at[1], below),
    ]
    hand = [remote(pad.at[l, ends], far.at[0, l], hand_s.at[l], far_r.at[0, l], mate) for l in range(5)]
    lend = [remote(pad.at[3 * i, ends], lent.at[i], lend_s.at[i], lend_r.at[i], mate) for i in range(2)]

    chip_before = at(b - 2, dx, dy)

    def down(src, side, l, n, device):
        return remote(src, far.at[side, l], chain_s.at[n], far_r.at[side, l], device)

    even_down = [down(pad.at[l, ends], 1, l, n, chip_before) for n, l in enumerate((1, 2, 4))]
    even_down += [down(far.at[0, l], 1, l, 2 + l, at(b - 1, dx, dy)) for l in (1, 2)]
    odd_down = [down(lent.at[i], 0, 3 * i, i, chip_before) for i in (0, 1)]
    odd_down += [down(pad.at[l, ends], 1, l, n, chip_before) for n, l in ((2, 0), (3, 3), (4, 4))]

    def start_first(when):
        groups = [
            (partner, cx_copies + x_copies),
            (above, [cy_copies[0], y_copies[0]]),
            (below, [cy_copies[1], y_copies[1]]),
        ]
        for device, copies in groups:

            @pl.when(when(device))
            def _(copies=copies):
                for copy in copies:
                    copy.start()

        @pl.when(when(mate) & (core == 1))
        def _():
            for l in (1, 2, 0, 3):
                hand[l].start()

        @pl.when(when(mate) & (core == 0))
        def _():
            for copy in lend:
                copy.start()

        @pl.when(when(chip_before) & (core == 0))
        def _():
            even_down[0].start()
            even_down[1].start()

    start_first(lambda device: jnp.logical_not(is_root(device)))

    row = lax.broadcasted_iota(jnp.int32, (8, 128), 0)

    def coefficients(l):
        here = [cf[k, l] * 0.5 for k in range(3)]
        for k in range(3):
            ct[k, l] = here[k]
        for n, k in ((3, 1), (4, 2)):
            ct[n, l] = (cf[k, l + 1] if l < 3 else cfx[k]) * 0.5
            if l > 0:
                ct[n + 2, l] = cf[k, l - 1] * 0.5
        for n, k in ((7, 0), (8, 2)):
            ct[n, l] = jnp.where(row == 7, pltpu.roll(cfy[1, k, l] * 0.5, 7, 0), pltpu.roll(here[k], 7, 0))
            ct[n + 2, l] = jnp.where(row == 0, pltpu.roll(cfy[0, k, l] * 0.5, 1, 0), pltpu.roll(here[k], 1, 0))
        for n, k in ((11, 0), (12, 1)):
            ct[n, l] = pltpu.roll(here[k], 127, 1)
            ct[n + 2, l] = pltpu.roll(here[k], 1, 1)

    rows = 32

    def fields_of(l):
        coefficients(l)

        def one_row(r, carry):
            c = [None if l == 0 and n in (5, 6) else jnp.broadcast_to(ct[n, l, pl.ds(r, 1), :], (rows, 128)) for n in range(15)]
            c1, c2, c3, c2xp, c3xp, c2xm, c3xm, c1yp, c3yp, c1ym, c3ym, c1zp, c2zp, c1zm, c2zm = c
            for j in range(128 // rows):
                part = pl.ds(j * rows, rows)
                mid = pad[l, r + 1, part, :].astype(F32)
                xp = pad[l + 1, r + 1, part, :].astype(F32)
                yp = pad[l, r + 2, part, :].astype(F32)
                ym = pad[l, r, part, :].astype(F32)
                zp = pltpu.roll(mid, 127, 1)
                zm = pltpu.roll(mid, 1, 1)
                g1, g2, g3 = xp, yp - ym, zp - zm
                c2x, c3x = c2xp * xp, c3xp * xp
                if l > 0:
                    xm = pad[l - 1, r + 1, part, :].astype(F32)
                    g1, c2x, c3x = g1 - xm, c2x - c2xm * xm, c3x - c3xm * xm
                uv[0, l, r, part, :] = (c2 * g3 - c3 * g2).astype(BF16)
                uv[1, l, r, part, :] = (c3 * g1 - c1 * g3).astype(BF16)
                uv[2, l, r, part, :] = (c1 * g2 - c2 * g1).astype(BF16)
                uv[3, l, r, part, :] = ((c3yp * yp - c3ym * ym) - (c2zp * zp - c2zm * zm)).astype(BF16)
                uv[4, l, r, part, :] = ((c1zp * zp - c1zm * zm) - c3x).astype(BF16)
                uv[5, l, r, part, :] = (c2x - (c1yp * yp - c1ym * ym)).astype(BF16)
            return carry

        lax.fori_loop(0, 8, one_row, 0)

    def fields_at_the_end():
        for n, k in ((0, 1), (1, 2)):
            ct[n, 4] = cfx[k] * 0.5

        def one_row(r, carry):
            c2, c3 = [jnp.broadcast_to(ct[n, 4, pl.ds(r, 1), :], (128, 128)) for n in (0, 1)]
            c2xm, c3xm = [jnp.broadcast_to(ct[n, 3, pl.ds(r, 1), :], (128, 128)) for n in (1, 2)]
            xm = pad[3, r + 1].astype(F32)
            uv[1, 4, r] = (-(c3 * xm)).astype(BF16)
            uv[2, 4, r] = (c2 * xm).astype(BF16)
            uv[4, 4, r] = (c3xm * xm).astype(BF16)
            uv[5, 4, r] = (-(c2xm * xm)).astype(BF16)
            return carry

        lax.fori_loop(0, 8, one_row, 0)

    def add(t, part, first):
        acc[t] = part if first else acc[t] + part

    def fields(k, l, end):
        return jnp.concatenate([wide(uv[k + i, l]) for i in range(1 if end else 0, 3)], axis=0)

    def add_own(l, first, end=False):
        part = lax.dot_general(fields(0, l, end), wide(pad[l, ends]), NT, preferred_element_type=F32)
        for i, k in enumerate((1, 2) if end else (0, 1, 2)):
            add(k, part[i * 128 : i * 128 + 128], first)

    def add_back(side, l, first, end=False):
        back = lax.dot_general(wide(far[side, l]), fields(3, l, end), NT, preferred_element_type=F32)
        for i, k in enumerate((1, 2) if end else (0, 1, 2)):
            add(6 + 6 * side + k, back[:, i * 128 : i * 128 + 128], first)

    def add_far(side, l, first, end=False):
        part = lax.dot_general(fields(0, l, end), wide(far[side, l]), NT, preferred_element_type=F32)
        for i, k in enumerate((1, 2) if end else (0, 1, 2)):
            add(3 + 6 * side + k, part[i * 128 : i * 128 + 128], first)

    def send_sums(group, first, count):
        for t in range(first, first + count):
            stage[t] = acc[t].astype(BF16).reshape(2, 4, 16, 128)
        tiles = pl.ds(first, count)
        copies = []
        for o in (2, 1, 3):
            copy = remote(
                stage.at[tiles, :, lax.rem(dy + o, 4)], from_dy.at[o - 1, tiles],
                sum_s.at[group, o - 1], sum_r.at[group, o - 1], at(b, dx, dy + o),
            )
            copy.start()
            copies.append(copy)
        return copies

    def sums(t, x):
        total = acc[t, pl.ds(pl.multiple_of((x * 4 + dy) * 16, 16), 16), :]
        for o in range(3):
            total = total + from_dy[o, t, x].astype(F32)
        return total

    other = 1 - dx
    home = []

    def send_home(copy):
        copy.start()
        home.append(copy)

    def to_partner(group, first):
        for k in range(3):
            half[3 * group + k] = sums(first + k, other)
        send_home(
            remote(
                half.at[pl.ds(3 * group, 3)], from_dx.at[group], home_s.at[group], home_r.at[group], partner
            )
        )

    def to_panel(side, first, landing):
        for x in (0, 1):
            for k in range(3):
                half[9 + 6 * side + 3 * x + k] = sums(first + k, x)
            send_home(
                remote(
                    half.at[pl.ds(9 + 6 * side + 3 * x, 3)], landing.at[dx],
                    home_s.at[3 + 2 * side + x], home_r.at[3 + 2 * side + dx], at(b + side + 1, x, dy),
                )
            )

    def arrived(copies):
        for copy in copies:
            copy.wait_recv()

    arrived(cy_copies + y_copies)
    fields_of(0)

    @pl.when(core == 1)
    def _():
        for i in (0, 1):
            lend[i].wait_recv()
            odd_down[i].start()
        odd_down[2].start()
        odd_down[3].start()

    fields_of(1)
    fields_of(2)

    @pl.when(near == 1)
    def _():
        pl.semaphore_wait(late, 1)
        start_first(is_root)

    @pl.when(core == 0)
    def _():
        for l in (1, 2):
            hand[l].wait_recv()
            even_down[2 + l].start()

    for l in range(3):
        add_own(l, l == 0)
    arrived(cx_copies + x_copies)

    @pl.when(core == 0)
    def _():
        even_down[2].start()

    @pl.when(core == 1)
    def _():
        odd_down[4].start()
        hand[4].start()

    fields_of(3)
    fields_at_the_end()
    add_own(3, False)
    add_own(4, False, True)
    first_sums = send_sums(0, 0, 3)

    places = [1 - core, 2 + core, core, 3 - core, 4]

    def take(side, n):
        l = places[n]
        pass_on = remote(
            far.at[side, l], far.at[1 - side, l], pass_s.at[min(n, 2) if n != 4 else 2], far_r.at[1 - side, l], mate
        )
        slot = remote(far.at[side, l], far.at[side, l], pass_s.at[0], far_r.at[side, l], mate)
        if side == 0:
            if n < 2:

                @pl.when(core == 1)
                def _():
                    slot.wait_recv()
                    pass_on.start()

            else:
                slot.wait_recv()
        else:
            slot.wait_recv()
            if n in (0, 1, 4):

                @pl.when(core == 0)
                def _():
                    pass_on.start()

        add_back(side, l, n == 0, n == 4)
        if side == 0 or n < 4:
            add_far(side, l, n == 0, n == 4)
        return pass_on

    passed = []
    for n in range(5):
        passed.append(take(0, n))
    one_sums = send_sums(1, 3, 6)
    arrived(first_sums)
    to_partner(0, 0)
    for n in range(4):
        take(1, n)
    arrived(one_sums)
    to_partner(1, 3)
    to_panel(0, 6, from_one)
    take(1, 4)
    back_sums = send_sums(2, 12, 3)
    add_far(1, 4, False, True)
    two_sums = send_sums(3, 9, 3)
    arrived(back_sums)
    to_panel(1, 12, from_two)
    arrived(two_sums)
    to_partner(2, 9)

    def waited(side, x, landing):
        copy = remote(
            half.at[pl.ds(9, 3)], landing.at[x], home_s.at[3 + 2 * side + x], home_r.at[3 + 2 * side + x], partner
        )
        copy.wait_recv()

    def own_rows(group, first):
        home[(0, 1, 6)[group]].wait_recv()
        for k in range(3):
            out[k, 2 + group] = (sums(first + k, dx) + from_dx[group, k]) * scale

    own_rows(0, 0)
    own_rows(1, 3)
    for x in (0, 1):
        waited(0, x, from_one)
    for k in range(3):
        out[k, 1] = (from_one[0, k] + from_one[1, k]) * scale
    own_rows(2, 9)
    for x in (0, 1):
        waited(1, x, from_two)
    for k in range(3):
        out[k, 0] = (from_two[0, k] + from_two[1, k]) * scale

    for copy in x_copies + cx_copies + y_copies + cy_copies + first_sums + one_sums + back_sums + two_sums + home + even_down:
        copy.wait_send()
    for n in (0, 1):
        passed[n].wait_send()

    @pl.when(core == 0)
    def _():
        passed[4].wait_send()
        for copy in lend:
            copy.wait_send()

    @pl.when(core == 1)
    def _():
        for copy in hand:
            copy.wait_send()


def on_device(n_blk, scale, orbitals, coupling, pot_grad):
    dma = pltpu.SemaphoreType.DMA
    vmem = pl.BlockSpec(memory_space=pltpu.VMEM)
    return pl.pallas_call(
        functools.partial(kernel, n_blk, scale),
        out_shape=jax.ShapeDtypeStruct((3, 5, 16, 128), F32),
        in_specs=[pl.BlockSpec(memory_space=pltpu.HBM)] * 3,
        out_specs=vmem,
        scratch_shapes=[
            pltpu.VMEM((128, 4, 8, 128), BF16),
            pltpu.VMEM((4, 8, 128), F32),
            pltpu.VMEM((3, 4, 8, 128), F32),
            pltpu.VMEM((4096, 128), F32),
            pltpu.VMEM((5, 10, 128, 128), BF16),
            pltpu.VMEM((3, 4, 8, 128), F32),
            pltpu.VMEM((3, 8, 128), F32),
            pltpu.VMEM((2, 3, 4, 8, 128), F32),
            pltpu.VMEM((15, 5, 8, 128), F32),
            pltpu.VMEM((6, 5, 8, 128, 128), BF16),
            pltpu.VMEM((2, 5, 8, 128, 128), BF16),
            pltpu.VMEM((2, 8, 128, 128), BF16),
            pltpu.VMEM((15, 128, 128), F32),
            pltpu.VMEM((15, 2, 4, 16, 128), BF16),
            pltpu.VMEM((3, 15, 2, 16, 128), BF16),
            pltpu.VMEM((21, 16, 128), F32),
            pltpu.VMEM((3, 3, 16, 128), F32),
            pltpu.VMEM((2, 3, 16, 128), F32),
            pltpu.VMEM((2, 3, 16, 128), F32),
            dma((3,)), dma, dma, dma((2,)), dma((2,)), dma, dma, dma((2,)), dma((2,)),
            dma((5,)), dma((2,)), dma((2,)), dma((5,)), dma((3,)), dma((2, 5)),
            dma((4, 3)), dma((4, 3)), dma((7,)), dma((7,)), pltpu.SemaphoreType.REGULAR,
        ],
        compiler_params=pltpu.CompilerParams(
            collective_id=0, has_side_effects=True, vmem_limit_bytes=67043328 - 128 * 1024
        ),
    )(orbitals, coupling, pot_grad)


def solution(mesh):
    cells = 8 * 32 * 128
    in_specs = (P("blk", "dx", "dy", None), P("dx", "dy", None), P(None, "dx", "dy", None))
    out_specs = P(None, None, ("blk", "dx", "dy"), None)
    return jax.shard_map(
        functools.partial(on_device, mesh.shape["blk"], 1.0 / math.sqrt(cells)),
        mesh=mesh, in_specs=in_specs, out_specs=out_specs, check_vma=False,
    )
```
